32 devices in a mesh: batch: 4 (over z), token: 8 (over y, x, core).
Axes of the slice: x: 2, y: 2, z: 4, core: 2. Of those that a mesh axis runs over, the one named last changes fastest.
Arguments:
- tokens: bfloat16 [16384, 768], P(('batch', 'token')), may hold values from -9 to 9
- slot_weight: bfloat16 [768, 1024], replicated, may hold values from -2 to 2
- expert_in: bfloat16 [128, 768, 3072], P('token', None, 'batch'), may hold values from -1.7265625 to 1.7265625
- expert_out: bfloat16 [128, 3072, 768], P('token', 'batch'), may hold values from -0.6484375 to 0.6484375
Outputs:
- mixed: bfloat16 [16384, 768], P(('batch', 'token'))
The draws below stay inside these ranges and needn't reach their ends.
All inputs are finite; a program needn't handle non-finite values.
Results may differ from the reference program's by a relative error of at most 0.023.
Values may be sent and summed in bfloat16 or wider, within the bound.
No kernel may reach another device: no remote copies, remote signals or barrier semaphores. Data moves between devices by JAX's collectives and lax.ppermute only.
A program may use at most 128 MiB of HBM per device.

```python
import jax
import jax.numpy as jnp
from jax import lax

D = 768
FF = 3072
EXPERTS = 128
SLOT_EACH = 8
GROUP_TOK = 4096
TOKENS = 16384
SLOTS = 1024
N_BATCH = 4


def draw_tokens(key, part):
    key_main, key_drift = jax.random.split(jax.random.fold_in(key, 3))
    values = jnp.clip(jax.random.normal(key_main, (TOKENS, D), jnp.float32), -4.0, 4.0)
    drift = jnp.clip(jax.random.normal(key_drift, (D,), jnp.float32), -3.0, 3.0)
    position = (jnp.arange(TOKENS) % GROUP_TOK).astype(jnp.float32) / GROUP_TOK
    values = values + (1.5 * position)[:, None] * drift[None, :]
    return values.astype(jnp.bfloat16)


def draw_slot_weight(key, part):
    scale_value = 2.0 / D ** 0.5
    values = jax.random.normal(jax.random.fold_in(key, 5), (D, SLOTS), jnp.float32) * scale_value
    values = jnp.clip(values, -4.0 * scale_value, 4.0 * scale_value)
    return values.astype(jnp.bfloat16)


def steps_of(own_key, extent, cuts, low, top_value):
    def one(dim, parts):
        draws = jax.random.uniform(jax.random.fold_in(jax.random.fold_in(own_key, 6), dim), (parts,), jnp.float32, low / len(cuts), top_value / len(cuts))
        return jnp.repeat(jnp.exp(draws), extent[dim] // parts).reshape((-1,) + (1,) * (len(extent) - dim - 1))

    factor_of = one(*cuts[0])
    for cut in cuts[1:]:
        factor_of = factor_of * one(*cut)
    return factor_of


def gaussian(key, extent, scale, bound, shards=(), kind=jnp.bfloat16):
    level = steps_of(key, extent, shards, -0.22, 0.18) if shards else 1.0
    entries = jax.random.normal(key, extent, jnp.float32) * scale * level
    return jnp.minimum(jnp.maximum(entries, -bound), bound).astype(kind)


def setup_inputs(seed: int = 0) -> dict:
    key_of = jax.random.split(jax.random.key(seed), 5)
    tokens = draw_tokens(jax.random.fold_in(key_of[4], 71), 0)
    slot_weight = draw_slot_weight(jax.random.fold_in(key_of[4], 71), 0)
    expert_in = gaussian(key_of[2], (EXPERTS, D, FF), (8.0 / D ** 0.5), 1.7265625, ((0, 8), (2, 4)))
    expert_out = gaussian(key_of[3], (EXPERTS, FF, D), (6.0 / FF ** 0.5), 0.6484375, ((0, 8), (1, 4)))
    return dict(tokens=tokens, slot_weight=slot_weight, expert_in=expert_in, expert_out=expert_out)


def normalize(rows_in):
    widened = rows_in.astype(jnp.float32)
    scale_row = lax.rsqrt(lax.optimization_barrier(jnp.mean(widened * widened, axis=-1, keepdims=True)) + 1e-06)
    return (widened * scale_row).astype(jnp.bfloat16)

def reference(tokens, slot_weight, expert_in, expert_out):
    groups = tokens.reshape(N_BATCH, GROUP_TOK, D)

    def first_pass(group_rows):
        normed = normalize(group_rows)
        logits = jnp.dot(normed, slot_weight, preferred_element_type=jnp.float32)
        column_max = lax.optimization_barrier(jnp.max(logits, axis=0))
        raised = jnp.exp(logits - column_max[None, :])
        column_sum = lax.optimization_barrier(jnp.sum(raised, axis=0))
        dispatch = raised.astype(jnp.bfloat16)
        slot_sum = jnp.dot(dispatch.T, normed, preferred_element_type=jnp.float32)
        return (slot_sum / column_sum[:, None]).astype(jnp.bfloat16)
    slot_inputs = lax.map(first_pass, groups)
    by_expert = slot_inputs.reshape(N_BATCH, EXPERTS, SLOT_EACH, D).transpose(1, 0, 2, 3)
    by_expert = by_expert.reshape(EXPERTS, N_BATCH * SLOT_EACH, D)

    def run_expert(packed):
        expert_rows, first_w, second_w = packed
        hidden = jnp.dot(expert_rows, first_w, preferred_element_type=jnp.float32)
        hidden = jax.nn.gelu(hidden, approximate=False).astype(jnp.bfloat16)
        blocks = hidden.reshape(N_BATCH * SLOT_EACH, N_BATCH, FF // N_BATCH).astype(jnp.float32)
        weights_blocks = second_w.reshape(N_BATCH, FF // N_BATCH, D).astype(jnp.float32)
        partials = jnp.einsum('rbf,bfd->brd', blocks, weights_blocks).astype(jnp.bfloat16)
        return lax.optimization_barrier(jnp.sum(partials.astype(jnp.float32), axis=0)).astype(jnp.bfloat16)
    expert_results = lax.map(run_expert, (by_expert, expert_in, expert_out))
    slot_outputs = expert_results.reshape(EXPERTS, N_BATCH, SLOT_EACH, D).transpose(1, 0, 2, 3)
    slot_outputs = slot_outputs.reshape(N_BATCH, SLOTS, D)

    def second_pass(packed):
        group_rows, group_outputs = packed
        normed = normalize(group_rows)
        logits = jnp.dot(normed, slot_weight, preferred_element_type=jnp.float32)
        combine = jax.nn.softmax(logits, axis=1).astype(jnp.bfloat16)
        return jnp.dot(combine, group_outputs, preferred_element_type=jnp.float32).astype(jnp.bfloat16)
    mixed = lax.map(second_pass, (groups, slot_outputs))
    return mixed.reshape(TOKENS, D)
```

```python
import functools

import jax
import jax.numpy as jnp
from jax import lax
from jax.experimental import pallas as pl
from jax.experimental.pallas import tpu as pltpu
from jax.sharding import PartitionSpec as P

F32, BF16 = jnp.float32, jnp.bfloat16
CHUNKS = 1
STATS = 8


def call(kernel, out_shape, *, flops, moved, name, **kw):
    return pl.pallas_call(
        kernel,
        out_shape=out_shape,
        cost_estimate=pl.CostEstimate(flops=int(flops), bytes_accessed=int(moved), transcendentals=0),
        name=name,
        **kw,
    )


def normalize_kernel(x_ref, out_ref):
    x = x_ref[...].astype(F32)
    scale = lax.rsqrt(jnp.mean(x * x, axis=-1, keepdims=True) + 1e-06)
    out_ref[...] = (x * scale).astype(BF16)


def normalize(x):
    return call(
        normalize_kernel,
        jax.ShapeDtypeStruct(x.shape, BF16),
        flops=4 * x.size,
        moved=4 * x.size,
        name="normalize",
    )(x)


def partial_kernel(which_ref, own_ref, other_ref, w_ref, out_ref):
    del which_ref
    w = w_ref[...].reshape(w_ref.shape[-2:])
    slots = w.shape[1]
    own, other = own_ref[...], other_ref[...]
    l0 = jnp.dot(own, w, preferred_element_type=F32)
    l1 = jnp.dot(other, w, preferred_element_type=F32)
    top = jnp.maximum(jnp.max(l0, axis=0, keepdims=True), jnp.max(l1, axis=0, keepdims=True))
    top = top.astype(BF16).astype(F32)
    e0, e1 = jnp.exp(l0 - top), jnp.exp(l1 - top)
    total = jnp.sum(e0, axis=0, keepdims=True) + jnp.sum(e1, axis=0, keepdims=True)
    dims = (((0,), (0,)), ((), ()))
    value = lax.dot_general(e0.astype(BF16), own, dims, preferred_element_type=F32)
    value += lax.dot_general(e1.astype(BF16), other, dims, preferred_element_type=F32)
    high = total.astype(BF16).astype(F32)
    row = lax.broadcasted_iota(jnp.int32, (STATS, slots), 0)
    stats = jnp.where(row == 0, top, jnp.where(row == 1, high, total - high))
    out_ref[:slots, :] = value.astype(BF16)
    out_ref[slots:, :] = jnp.zeros((STATS, out_ref.shape[1]), BF16)
    out_ref[slots:, :slots] = stats.astype(BF16)


def partial(which, own, other, weight, slots):
    rows, width = own.shape
    whole = lambda i, which_ref: (0, 0)
    if weight.ndim == 2:
        w_spec = pl.BlockSpec((width, slots), lambda i, which_ref: (0, which_ref[0]))
    else:
        w_spec = pl.BlockSpec((1, width, slots), lambda i, which_ref: (which_ref[0], 0, 0))
    return call(
        partial_kernel,
        jax.ShapeDtypeStruct((slots + STATS, width), BF16),
        flops=8 * rows * width * slots,
        moved=4 * rows * width,
        name="partial",
        grid_spec=pltpu.PrefetchScalarGridSpec(
            num_scalar_prefetch=1,
            grid=(1,),
            in_specs=[pl.BlockSpec((rows, width), whole)] * 2 + [w_spec],
            out_specs=pl.BlockSpec((slots + STATS, width), whole),
        ),
    )(which, own, other, weight)


def combine_kernel(count, *refs):
    parts, out_ref = refs[:count], refs[count]
    slots = out_ref.shape[0]
    tops = [p[slots : slots + 1, :slots].astype(F32) for p in parts]
    totals = [
        p[slots + 1 : slots + 2, :slots].astype(F32) + p[slots + 2 : slots + 3, :slots].astype(F32)
        for p in parts
    ]
    top = functools.reduce(jnp.maximum, tops)
    factors = [jnp.exp(t - top) for t in tops]
    total = sum(f * t for f, t in zip(factors, totals))
    inverse = 1.0 / total
    shape = (slots, slots)
    eye = lax.broadcasted_iota(jnp.int32, shape, 0) == lax.broadcasted_iota(jnp.int32, shape, 1)
    value = 0.0
    for f, p in zip(factors, parts):
        column = jnp.sum(jnp.where(eye, f * inverse, 0.0), axis=1, keepdims=True)
        value = value + p[:slots, :].astype(F32) * column
    out_ref[...] = value.astype(BF16)


def combine(parts, slots):
    width = parts[0].shape[1]
    return call(
        functools.partial(combine_kernel, len(parts)),
        jax.ShapeDtypeStruct((slots, width), BF16),
        flops=4 * len(parts) * slots * width,
        moved=2 * len(parts) * slots * width,
        name="combine",
    )(*parts)


def softmax_kernel(x_ref, w_ref, out_ref):
    logits = jnp.dot(x_ref[...], w_ref[...], preferred_element_type=F32)
    raised = jnp.exp(logits - jnp.max(logits, axis=1, keepdims=True))
    out_ref[...] = (raised / jnp.sum(raised, axis=1, keepdims=True)).astype(BF16)


def softmax(x, weight):
    rows, width = x.shape
    slots = weight.shape[1]
    step = min(rows, 128)
    return call(
        softmax_kernel,
        jax.ShapeDtypeStruct((rows, slots), BF16),
        flops=2 * rows * width * slots,
        moved=2 * (rows * width + width * slots + rows * slots),
        name="softmax",
        grid=(rows // step,),
        in_specs=[
            pl.BlockSpec((step, width), lambda i: (i, 0)),
            pl.BlockSpec((width, slots), lambda i: (0, 0)),
        ],
        out_specs=pl.BlockSpec((step, slots), lambda i: (i, 0)),
    )(x, weight)


def expert_kernel(count, *refs):
    xs, w_in, w_out, ys = refs[:count], refs[count], refs[count + 1], refs[count + 2 :]
    each = xs[0].shape[0]
    rows = jnp.concatenate([x[...] for x in xs], axis=0)
    hidden = jnp.dot(rows, w_in[0], preferred_element_type=F32)
    hidden = (0.5 * hidden * (1.0 + lax.erf(hidden * 0.7071067811865476))).astype(BF16)
    terms = jnp.dot(hidden, w_out[0], preferred_element_type=F32)
    for k, y in enumerate(ys):
        y[...] = terms[k * each : (k + 1) * each].astype(BF16)


def experts(xs, w_in, w_out, first, count):
    rows, width = xs[0].shape
    each = rows // count
    hidden = w_in.shape[2]
    row_spec = pl.BlockSpec((each, width), lambda e: (e, 0))
    return call(
        functools.partial(expert_kernel, len(xs)),
        [jax.ShapeDtypeStruct((rows, width), BF16)] * len(xs),
        flops=4 * len(xs) * rows * width * hidden,
        moved=4 * count * width * hidden,
        name="experts",
        grid=(count,),
        in_specs=[row_spec] * len(xs)
        + [
            pl.BlockSpec((1, width, hidden), lambda e: (first + e, 0, 0)),
            pl.BlockSpec((1, hidden, width), lambda e: (first + e, 0, 0)),
        ],
        out_specs=[row_spec] * len(xs),
    )(*xs, w_in, w_out)


def total_kernel(count, *refs):
    refs[count][...] = sum(r[...].astype(F32) for r in refs[:count]).astype(BF16)


def add_up(parts):
    rows, width = parts[0].shape
    return call(
        functools.partial(total_kernel, len(parts)),
        jax.ShapeDtypeStruct((rows, width), BF16),
        flops=len(parts) * rows * width,
        moved=2 * len(parts) * rows * width,
        name="add_up",
    )(*parts)


def mix_kernel(count, chunks, at_ref, c_ref, *refs):
    blocks, out_ref, held = refs[:count], refs[count], refs[count + 1]
    span = blocks[0].shape[0]
    for n, block in enumerate(blocks):
        j, chunk = n % (count // chunks), n // (count // chunks)
        start = pl.multiple_of(at_ref[j] * (span * chunks) + chunk * span, 8)
        held[pl.ds(start, span), :] = block[...]
    out_ref[...] = jnp.dot(c_ref[...], held[...], preferred_element_type=F32).astype(BF16)


def mix(at, weights, blocks, chunks):
    rows, slots = weights.shape
    span, width = blocks[0].shape
    whole = lambda i, at_ref: (0, 0)
    return call(
        functools.partial(mix_kernel, len(blocks), chunks),
        jax.ShapeDtypeStruct((rows, width), BF16),
        flops=2 * rows * slots * width,
        moved=2 * (rows * slots + slots * width + rows * width),
        name="mix",
        grid_spec=pltpu.PrefetchScalarGridSpec(
            num_scalar_prefetch=1,
            grid=(1,),
            in_specs=[pl.BlockSpec((rows, slots), whole)]
            + [pl.BlockSpec((span, width), whole)] * len(blocks),
            out_specs=pl.BlockSpec((rows, width), whole),
            scratch_shapes=[pltpu.VMEM((slots, width), BF16)],
        ),
    )(at, weights, *blocks)


def body(tokens, slot_weight, expert_in, expert_out):
    n_token, n_batch = lax.axis_size("token"), lax.axis_size("batch")
    me = lax.axis_index("token")
    chips = n_token // 2
    experts_here = expert_in.shape[0]
    slots = slot_weight.shape[1] // n_token
    width = tokens.shape[1]

    def over_token(x, k):
        return lax.ppermute(x, "token", [(i, i ^ k) for i in range(n_token)])

    def over_batch(x, k):
        return lax.ppermute(x, "batch", [(i, i ^ k) for i in range(n_batch)])

    own = normalize(tokens)
    other = over_token(own, 1)
    if slots % 128:
        weight = slot_weight.reshape(width, n_token, slots).transpose(1, 0, 2)
    else:
        weight = slot_weight
    arrived = []
    for k in reversed(range(chips)):
        which = jnp.bitwise_xor(me, 2 * k).astype(jnp.int32)[None]
        sent = partial(which, own, other, weight, slots)
        arrived.append(over_token(sent, 2 * k) if k else sent)
    slot_inputs = combine(arrived, slots)
    weights = softmax(own, slot_weight)

    chunk_experts = experts_here // CHUNKS
    span = slots // CHUNKS
    blocks = []
    for c in range(CHUNKS):
        mine = slot_inputs[c * span : (c + 1) * span]
        xs = [over_batch(mine, k) if k else mine for k in reversed(range(n_batch))]
        ys = experts(xs, expert_in, expert_out, c * chunk_experts, chunk_experts)
        parts = [over_batch(y, k) if k else y for k, y in zip(reversed(range(n_batch)), ys)]
        rows = add_up(parts)
        there = [over_token(rows, 2 * k) if k else rows for k in range(chips)]
        blocks += there + [over_token(r, 1) for r in there]
    order = [2 * k for k in range(chips)] + [2 * k + 1 for k in range(chips)]
    at = jnp.bitwise_xor(me, jnp.array(order, jnp.int32))
    return mix(at, weights, blocks, CHUNKS)


def solution(mesh):
    placed = (
        P(("batch", "token"), None),
        P(),
        P("token", None, "batch"),
        P("token", "batch", None),
    )
    return jax.shard_map(
        body, mesh=mesh, in_specs=placed, out_specs=P(("batch", "token"), None), check_vma=False
    )
```

```python
import functools

import jax
import jax.numpy as jnp
from jax import lax
from jax.experimental import pallas as pl
from jax.experimental.pallas import tpu as pltpu
from jax.sharding import PartitionSpec as P

F32, BF16 = jnp.float32, jnp.bfloat16
CHUNKS = 1
STATS = 8


def in_vmem(x):
    return pltpu.with_memory_space_constraint(x, pltpu.VMEM)


def call(kernel, shapes, operands, *, moved, name, scalars=0, scratch=(), limit=8 << 20):
    many = isinstance(shapes, list)
    shapes = shapes if many else [shapes]
    scalar, place = pl.BlockSpec(memory_space=pltpu.SMEM), pl.BlockSpec(memory_space=pltpu.VMEM)
    results = pl.pallas_call(
        kernel,
        out_shape=[pltpu.VMEM(shape, BF16) for shape in shapes],
        in_specs=[scalar] * scalars + [place] * (len(operands) - scalars),
        out_specs=[place] * len(shapes),
        scratch_shapes=scratch,
        cost_estimate=pl.CostEstimate(flops=int(1e11), bytes_accessed=int(moved), transcendentals=0),
        compiler_params=pltpu.CompilerParams(vmem_limit_bytes=limit),
        name=name,
    )(*operands[:scalars], *[in_vmem(x) for x in operands[scalars:]])
    return results if many else results[0]


def normalize_kernel(x_ref, out_ref):
    x = x_ref[...].astype(F32)
    scale = lax.rsqrt(jnp.mean(x * x, axis=-1, keepdims=True) + 1e-06)
    out_ref[...] = (x * scale).astype(BF16)


def normalize(x):
    return call(normalize_kernel, x.shape, [x], moved=4 * x.size, name="normalize")


def partial_kernel(which_ref, own_ref, other_ref, w_ref, out_ref):
    slots = out_ref.shape[0] - STATS
    if len(w_ref.shape) == 2:
        w = w_ref[:, pl.ds(pl.multiple_of(which_ref[0] * slots, slots), slots)]
    else:
        w = w_ref[which_ref[0]]
    own, other = own_ref[...], other_ref[...]
    l0 = jnp.dot(own, w, preferred_element_type=F32)
    l1 = jnp.dot(other, w, preferred_element_type=F32)
    top = jnp.maximum(jnp.max(l0, axis=0, keepdims=True), jnp.max(l1, axis=0, keepdims=True))
    top = top.astype(BF16).astype(F32)
    e0, e1 = jnp.exp(l0 - top), jnp.exp(l1 - top)
    total = jnp.sum(e0, axis=0, keepdims=True) + jnp.sum(e1, axis=0, keepdims=True)
    dims = (((0,), (0,)), ((), ()))
    value = lax.dot_general(e0.astype(BF16), own, dims, preferred_element_type=F32)
    value += lax.dot_general(e1.astype(BF16), other, dims, preferred_element_type=F32)
    high = total.astype(BF16).astype(F32)
    row = lax.broadcasted_iota(jnp.int32, (STATS, slots), 0)
    stats = jnp.where(row == 0, top, jnp.where(row == 1, high, total - high))
    out_ref[:slots, :] = value.astype(BF16)
    out_ref[slots:, :] = jnp.zeros((STATS, out_ref.shape[1]), BF16)
    out_ref[slots:, :slots] = stats.astype(BF16)


def partial(which, own, other, weight, slots):
    rows, width = own.shape
    return call(
        partial_kernel,
        (slots + STATS, width),
        [which, own, other, weight],
        moved=4 * rows * width,
        name="partial",
        scalars=1,
    )


def combine_kernel(count, *refs):
    parts, out_ref = refs[:count], refs[count]
    slots = out_ref.shape[0]
    tops = [p[slots : slots + 1, :slots].astype(F32) for p in parts]
    totals = [
        p[slots + 1 : slots + 2, :slots].astype(F32) + p[slots + 2 : slots + 3, :slots].astype(F32)
        for p in parts
    ]
    top = functools.reduce(jnp.maximum, tops)
    factors = [jnp.exp(t - top) for t in tops]
    total = sum(f * t for f, t in zip(factors, totals))
    inverse = 1.0 / total
    shape = (slots, slots)
    eye = lax.broadcasted_iota(jnp.int32, shape, 0) == lax.broadcasted_iota(jnp.int32, shape, 1)
    value = 0.0
    for f, p in zip(factors, parts):
        column = jnp.sum(jnp.where(eye, f * inverse, 0.0), axis=1, keepdims=True)
        value = value + p[:slots, :].astype(F32) * column
    out_ref[...] = value.astype(BF16)


def combine(parts, slots):
    width = parts[0].shape[1]
    return call(
        functools.partial(combine_kernel, len(parts)),
        (slots, width),
        parts,
        moved=2 * len(parts) * slots * width,
        name="combine",
    )


def softmax_kernel(step, x_ref, w_ref, out_ref):
    @pl.loop(0, x_ref.shape[0] // step)
    def _(i):
        rows = pl.ds(pl.multiple_of(i * step, step), step)
        logits = jnp.dot(x_ref[rows, :], w_ref[...], preferred_element_type=F32)
        raised = jnp.exp(logits - jnp.max(logits, axis=1, keepdims=True))
        out_ref[rows, :] = (raised / jnp.sum(raised, axis=1, keepdims=True)).astype(BF16)


def softmax(x, weight):
    rows, width = x.shape
    slots = weight.shape[1]
    return call(
        functools.partial(softmax_kernel, min(rows, 256)),
        (rows, slots),
        [x, weight],
        moved=2 * (rows * width + width * slots + rows * slots),
        name="softmax",
    )


def expert_kernel(count, first, n, each, *refs):
    xs, w_in, w_out, ys = refs[:count], refs[count], refs[count + 1], refs[count + 2 :]

    @pl.loop(0, n)
    def _(e):
        at = pl.ds(pl.multiple_of(e * each, each), each)
        rows = jnp.concatenate([x[at, :] for x in xs], axis=0)
        hidden = jnp.dot(rows, w_in[first + e], preferred_element_type=F32)
        hidden = (0.5 * hidden * (1.0 + lax.erf(hidden * 0.7071067811865476))).astype(BF16)
        terms = jnp.dot(hidden, w_out[first + e], preferred_element_type=F32)
        for k, y in enumerate(ys):
            y[at, :] = terms[k * each : (k + 1) * each].astype(BF16)


def experts(xs, w_in, w_out, first, count):
    rows, width = xs[0].shape
    hidden = w_in.shape[2]
    return call(
        functools.partial(expert_kernel, len(xs), first, count, rows // count),
        [(rows, width)] * len(xs),
        [*xs, w_in, w_out],
        moved=4 * count * width * hidden,
        name="experts",
    )


def total_kernel(count, *refs):
    refs[count][...] = sum(r[...].astype(F32) for r in refs[:count]).astype(BF16)


def add_up(parts):
    rows, width = parts[0].shape
    return call(
        functools.partial(total_kernel, len(parts)),
        (rows, width),
        parts,
        moved=2 * len(parts) * rows * width,
        name="add_up",
    )


def mix_kernel(count, chunks, at_ref, c_ref, *refs):
    blocks, out_ref, held = refs[:count], refs[count], refs[count + 1]
    span = blocks[0].shape[0]
    for n, block in enumerate(blocks):
        j, chunk = n % (count // chunks), n // (count // chunks)
        start = pl.multiple_of(at_ref[j] * (span * chunks) + chunk * span, 8)
        held[pl.ds(start, span), :] = block[...]
    out_ref[...] = jnp.dot(c_ref[...], held[...], preferred_element_type=F32).astype(BF16)


def mix(at, weights, blocks, chunks):
    rows, slots = weights.shape
    width = blocks[0].shape[1]
    return call(
        functools.partial(mix_kernel, len(blocks), chunks),
        (rows, width),
        [at, weights, *blocks],
        moved=2 * (rows * slots + slots * width + rows * width),
        name="mix",
        scalars=1,
        scratch=[pltpu.VMEM((slots, width), BF16)],
    )


def body(tokens, slot_weight, expert_in, expert_out):
    n_token, n_batch = lax.axis_size("token"), lax.axis_size("batch")
    me = lax.axis_index("token")
    chips = n_token // 2
    experts_here = expert_in.shape[0]
    slots = slot_weight.shape[1] // n_token
    width = tokens.shape[1]

    def over_token(x, k):
        return lax.ppermute(x, "token", [(i, i ^ k) for i in range(n_token)])

    def over_batch(x, k):
        return lax.ppermute(x, "batch", [(i, i ^ k) for i in range(n_batch)])

    own = normalize(tokens)
    other = over_token(own, 1)
    if slots % 128:
        weight = slot_weight.reshape(width, n_token, slots).transpose(1, 0, 2)
    else:
        weight = slot_weight
    arrived = []
    for k in reversed(range(chips)):
        which = jnp.bitwise_xor(me, 2 * k).astype(jnp.int32)[None]
        sent = partial(which, own, other, weight, slots)
        arrived.append(over_token(sent, 2 * k) if k else sent)
    slot_inputs = combine(arrived, slots)
    weights = softmax(own, slot_weight)

    chunk_experts = experts_here // CHUNKS
    span = slots // CHUNKS
    blocks = []
    for c in range(CHUNKS):
        mine = slot_inputs[c * span : (c + 1) * span]
        xs = [over_batch(mine, k) if k else mine for k in reversed(range(n_batch))]
        ys = experts(xs, expert_in, expert_out, c * chunk_experts, chunk_experts)
        parts = [over_batch(y, k) if k else y for k, y in zip(reversed(range(n_batch)), ys)]
        rows = add_up(parts)
        there = [over_token(rows, 2 * k) if k else rows for k in range(chips)]
        blocks += there + [over_token(r, 1) for r in there]
    order = [2 * k for k in range(chips)] + [2 * k + 1 for k in range(chips)]
    at = jnp.bitwise_xor(me, jnp.array(order, jnp.int32))
    return mix(at, weights, blocks, CHUNKS)


def solution(mesh):
    placed = (
        P(("batch", "token"), None),
        P(),
        P("token", None, "batch"),
        P("token", "batch", None),
    )
    return jax.shard_map(
        body, mesh=mesh, in_specs=placed, out_specs=P(("batch", "token"), None), check_vma=False
    )
```

```python
import functools

import jax
import jax.numpy as jnp
from jax import lax
from jax.experimental import pallas as pl
from jax.experimental.pallas import tpu as pltpu
from jax.sharding import PartitionSpec as P


F32, BF16 = jnp.float32, jnp.bfloat16
CHUNKS = 2
SPLIT_SUMS = False
STATS = 8


def in_vmem(x):
    return pltpu.with_memory_space_constraint(x, pltpu.VMEM)


def call(kernel, shapes, operands, *, moved, scalars=0, scratch=(), dtype=BF16, hint=1e11, limit=8 << 20):
    many = isinstance(shapes, list)
    shapes = shapes if many else [shapes]
    scalar, place = pl.BlockSpec(memory_space=pltpu.SMEM), pl.BlockSpec(memory_space=pltpu.VMEM)
    results = pl.pallas_call(
        kernel,
        out_shape=[pltpu.VMEM(shape, dtype) for shape in shapes],
        in_specs=[scalar] * scalars + [place] * (len(operands) - scalars),
        out_specs=[place] * len(shapes),
        scratch_shapes=scratch,
        cost_estimate=pl.CostEstimate(flops=int(hint), bytes_accessed=int(moved), transcendentals=0),
        compiler_params=pltpu.CompilerParams(vmem_limit_bytes=limit),
    )(*operands[:scalars], *[in_vmem(x) for x in operands[scalars:]])
    return results if many else results[0]


def normalize_kernel(x_ref, out_ref):
    x = x_ref[...].astype(F32)
    scale = lax.rsqrt(jnp.mean(x * x, axis=-1, keepdims=True) + 1e-06)
    out_ref[...] = (x * scale).astype(BF16)


def normalize(x):
    return call(normalize_kernel, x.shape, [x], moved=4 * x.size)


def partial_kernel(slots, first, which_ref, own_ref, other_ref, w_ref, *out_refs):
    if len(w_ref.shape) == 2:
        w = w_ref[:, pl.ds(pl.multiple_of(which_ref[0] * slots, slots), slots)]
    else:
        w = w_ref[which_ref[0]]
    span = out_refs[0].shape[0] - STATS
    count = span * len(out_refs)
    if count < slots:
        w = w[:, first : first + count]
    own, other = own_ref[...], other_ref[...]
    l0 = jnp.dot(own, w, preferred_element_type=F32)
    l1 = jnp.dot(other, w, preferred_element_type=F32)
    top = jnp.maximum(jnp.max(l0, axis=0, keepdims=True), jnp.max(l1, axis=0, keepdims=True))
    top = top.astype(BF16).astype(F32)
    e0, e1 = jnp.exp(l0 - top), jnp.exp(l1 - top)
    total = jnp.sum(e0, axis=0, keepdims=True) + jnp.sum(e1, axis=0, keepdims=True)
    dims = (((0,), (0,)), ((), ()))
    value = lax.dot_general(e0.astype(BF16), own, dims, preferred_element_type=F32)
    value += lax.dot_general(e1.astype(BF16), other, dims, preferred_element_type=F32)
    high = total.astype(BF16).astype(F32)
    row = lax.broadcasted_iota(jnp.int32, (STATS, count), 0)
    stats = jnp.where(row == 0, top, jnp.where(row == 1, high, total - high)).astype(BF16)
    value = value.astype(BF16)
    for n, out_ref in enumerate(out_refs):
        part = slice(n * span, (n + 1) * span)
        out_ref[:span, :] = value[part]
        out_ref[span:, :] = jnp.zeros((STATS, out_ref.shape[1]), BF16)
        out_ref[span:, :span] = stats[:, part]


def partial(which, own, other, weight, slots, first, spans):
    rows, width = own.shape
    return call(
        functools.partial(partial_kernel, slots, first),
        [(span + STATS, width) for span in spans],
        [which, own, other, weight],
        moved=4 * rows * width,
        scalars=1,
    )


def combine_kernel(count, *refs):
    parts, out_refs = refs[:count], refs[count:]
    span = out_refs[0].shape[0]
    slots = span * len(out_refs)
    tops = [p[slots : slots + 1, :slots].astype(F32) for p in parts]
    totals = [
        p[slots + 1 : slots + 2, :slots].astype(F32) + p[slots + 2 : slots + 3, :slots].astype(F32)
        for p in parts
    ]
    top = functools.reduce(jnp.maximum, tops)
    factors = [jnp.exp(t - top) for t in tops]
    total = sum(f * t for f, t in zip(factors, totals))
    inverse = 1.0 / total
    shape = (slots, slots)
    eye = lax.broadcasted_iota(jnp.int32, shape, 0) == lax.broadcasted_iota(jnp.int32, shape, 1)
    value = 0.0
    for f, p in zip(factors, parts):
        column = jnp.sum(jnp.where(eye, f * inverse, 0.0), axis=1, keepdims=True)
        value = value + p[:slots, :].astype(F32) * column
    value = value.astype(BF16)
    for n, out_ref in enumerate(out_refs):
        out_ref[...] = value[n * span : (n + 1) * span]


def combine(parts, slots, chunks):
    width = parts[0].shape[1]
    return call(
        functools.partial(combine_kernel, len(parts)),
        [(slots // chunks, width)] * chunks,
        parts,
        moved=2 * len(parts) * slots * width,
    )


def softmax_kernel(step, span, x_ref, w_ref, *out_refs):
    chunks = len(out_refs)

    @pl.loop(0, x_ref.shape[0] // step)
    def _(i):
        rows = pl.ds(pl.multiple_of(i * step, step), step)
        logits = jnp.dot(x_ref[rows, :], w_ref[...], preferred_element_type=F32)
        raised = jnp.exp(logits - jnp.max(logits, axis=1, keepdims=True))
        share = raised / jnp.sum(raised, axis=1, keepdims=True)
        for c, out_ref in enumerate(out_refs):
            pieces = [
                share[:, at : at + span] for at in range(c * span, share.shape[1], chunks * span)
            ]
            out_ref[rows, :] = jnp.concatenate(pieces, axis=1).astype(BF16)


def softmax(x, weight, span, chunks):
    rows, width = x.shape
    slots = weight.shape[1]
    return call(
        functools.partial(softmax_kernel, min(rows, 256), span),
        [(rows, slots // chunks)] * chunks,
        [x, weight],
        moved=2 * (rows * width + width * slots + rows * slots),
    )


def in_hbm(x):
    return pltpu.with_memory_space_constraint(x, pltpu.HBM)


def load_kernel(parts, *refs):
    n = len(parts)
    copies = []
    for i, (first, count) in enumerate(parts):
        copies.append(
            pltpu.make_async_copy(refs[i].at[pl.ds(first, count)], refs[n + i], refs[2 * n].at[i])
        )
        copies[-1].start()
    for copy in copies:
        copy.wait()


def load(weights, parts):
    return pl.pallas_call(
        functools.partial(load_kernel, parts),
        out_shape=[
            pltpu.VMEM((count,) + w.shape[1:], BF16) for w, (_, count) in zip(weights, parts)
        ],
        in_specs=[pl.BlockSpec(memory_space=pl.ANY)] * len(parts),
        out_specs=[pl.BlockSpec(memory_space=pltpu.VMEM)] * len(parts),
        scratch_shapes=[pltpu.SemaphoreType.DMA((len(parts),))],
        cost_estimate=pl.CostEstimate(flops=int(1e9), bytes_accessed=1, transcendentals=0),
        compiler_params=pltpu.CompilerParams(vmem_limit_bytes=1 << 20),
        name="load",
    )(*[in_hbm(w) for w in weights])


def expert_kernel(count, n, each, first, *refs):
    xs, w_in, w_out = refs[:count], refs[count], refs[count + 1]
    if first is None:
        ys = refs[-count:]
        fetch = lambda e: []
    else:
        far_out = w_out
        w_out, sems = refs[-2:]
        ys = refs[-count - 2 : -2]

        def fetch(e):
            return [pltpu.make_async_copy(far_out.at[first + e], w_out.at[e], sems.at[e])]

        for e in range(n):
            for copy in fetch(e):
                copy.start()

    @pl.loop(0, n)
    def _(e):
        at = pl.ds(pl.multiple_of(e * each, each), each)
        rows = jnp.concatenate([x[at, :] for x in xs], axis=0)
        hidden = jnp.dot(rows, w_in[e], preferred_element_type=F32)
        hidden = (0.5 * hidden * (1.0 + lax.erf(hidden * 0.7071067811865476))).astype(BF16)
        for copy in fetch(e):
            copy.wait()
        terms = jnp.dot(hidden, w_out[e], preferred_element_type=F32)
        for k, y in enumerate(ys):
            y[at, :] = terms[k * each : (k + 1) * each].astype(BF16)


def experts(xs, w_in, w_out, first, count):
    rows, width = xs[0].shape
    hidden = w_in.shape[2]
    near = pl.BlockSpec(memory_space=pltpu.VMEM)
    far = first is not None
    scratch = [
        pltpu.VMEM((count, hidden, width), BF16),
        pltpu.SemaphoreType.DMA((count,)),
    ]
    return pl.pallas_call(
        functools.partial(expert_kernel, len(xs), count, rows // count, first),
        out_shape=[pltpu.VMEM((rows, width), BF16)] * len(xs),
        in_specs=[near] * (len(xs) + 1) + [pl.BlockSpec(memory_space=pl.ANY) if far else near],
        out_specs=[near] * len(xs),
        scratch_shapes=scratch if far else [],
        cost_estimate=pl.CostEstimate(flops=int(1e9), bytes_accessed=1, transcendentals=0),
        compiler_params=pltpu.CompilerParams(
            vmem_limit_bytes=(4 << 20) + (2 * count * width * hidden if far else 0)
        ),
        name="experts",
    )(*[in_vmem(x) for x in xs], in_vmem(w_in), in_hbm(w_out) if far else in_vmem(w_out))


def total_kernel(count, *refs):
    refs[count][...] = sum(r[...].astype(F32) for r in refs[:count]).astype(BF16)


def add_up(parts):
    rows, width = parts[0].shape
    return call(
        functools.partial(total_kernel, len(parts)),
        (rows, width),
        parts,
        moved=2 * len(parts) * rows * width,
    )


def place_rows(at_ref, blocks, held):
    span = blocks[0].shape[0]
    for j, block in enumerate(blocks):
        held[pl.ds(pl.multiple_of(at_ref[j] * span, 8), span), :] = block[...]


def first_mix_kernel(at_ref, c_ref, *refs):
    *blocks, out_ref, held = refs
    place_rows(at_ref, blocks, held)
    out_ref[...] = jnp.dot(c_ref[...], held[...], preferred_element_type=F32)


def last_mix_kernel(steps, at_ref, c_ref, sum_ref, *refs):
    *blocks, out_ref, held, made, sems = refs
    place_rows(at_ref, blocks, held)
    step = c_ref.shape[0] // steps
    copies = []
    for i in range(steps):
        rows = pl.ds(i * step, step)
        total = sum_ref[rows, :] + jnp.dot(c_ref[rows, :], held[...], preferred_element_type=F32)
        made[rows, :] = total.astype(BF16)
        copies.append(pltpu.make_async_copy(made.at[rows, :], out_ref.at[rows, :], sems.at[i]))
        copies[-1].start()
    for copy in copies:
        copy.wait()


def first_mix(at, weights, blocks):
    rows, slots = weights.shape
    width = blocks[0].shape[1]
    return call(
        first_mix_kernel,
        (rows, width),
        [at, weights, *blocks],
        moved=2 * (rows * slots + slots * width + rows * width),
        scalars=1,
        scratch=[pltpu.VMEM((slots, width), BF16)],
        dtype=F32,
    )


def last_mix(at, weights, before, blocks):
    rows, slots = weights.shape
    width = blocks[0].shape[1]
    steps = 4
    place = pl.BlockSpec(memory_space=pltpu.VMEM)
    return pl.pallas_call(
        functools.partial(last_mix_kernel, steps),
        out_shape=jax.ShapeDtypeStruct((rows, width), BF16),
        in_specs=[pl.BlockSpec(memory_space=pltpu.SMEM)] + [place] * (len(blocks) + 2),
        out_specs=pl.BlockSpec(memory_space=pl.ANY),
        scratch_shapes=[
            pltpu.VMEM((slots, width), BF16),
            pltpu.VMEM((rows, width), BF16),
            pltpu.SemaphoreType.DMA((steps,)),
        ],
        compiler_params=pltpu.CompilerParams(vmem_limit_bytes=8 << 20),
        name="last_mix",
    )(at, in_vmem(weights), in_vmem(before), *[in_vmem(b) for b in blocks])


def body(tokens, slot_weight, expert_in, expert_out):
    n_token, n_batch = lax.axis_size("token"), lax.axis_size("batch")
    me = lax.axis_index("token")
    chips = n_token // 2
    experts_here = expert_in.shape[0]
    slots = slot_weight.shape[1] // n_token
    width = tokens.shape[1]
    chunk_experts, span = experts_here // CHUNKS, slots // CHUNKS

    def over_token(x, k):
        return lax.ppermute(x, "token", [(i, i ^ k) for i in range(n_token)])

    def over_batch(x, k):
        return lax.ppermute(x, "batch", [(i, i ^ k) for i in range(n_batch)])

    other = normalize(over_token(tokens, 1))
    own = normalize(tokens)
    if slots % 128:
        weight = slot_weight.reshape(width, n_token, slots).transpose(1, 0, 2)
    else:
        weight = slot_weight
    here, there = (0, chunk_experts), (chunk_experts, chunk_experts)
    (in0,) = load([expert_in], [here])
    out0, in1 = load([expert_out, expert_in], [here, there])
    ins = [in0, in1]
    groups = [[c] for c in range(CHUNKS)] if SPLIT_SUMS else [list(range(CHUNKS))]
    inputs = []
    for group in groups:
        arrived = []
        count = span * len(group)
        for k in reversed(range(chips)):
            which = jnp.bitwise_xor(me, 2 * k).astype(jnp.int32)[None]
            (sent,) = partial(which, own, other, weight, slots, group[0] * span, [count])
            arrived.append(over_token(sent, 2 * k) if k else sent)
        inputs += combine(arrived, count, len(group))
    weights = softmax(own, slot_weight, span, CHUNKS)

    order = [2 * k for k in range(chips)] + [2 * k + 1 for k in range(chips)]
    at = jnp.bitwise_xor(me, jnp.array(order, jnp.int32))
    xs = []
    for x in inputs:
        xs.append([over_batch(x, k) if k else x for k in reversed(range(n_batch))])
    parts = []
    for c in range(CHUNKS):
        far = c * chunk_experts if c else None
        ys = experts(xs[c], ins[c], expert_out if c else out0, far, chunk_experts)
        parts.append([over_batch(y, k) if k else y for k, y in zip(reversed(range(n_batch)), ys)])
    total = None
    for c in range(CHUNKS):
        rows = add_up(parts[c])
        there = [over_token(rows, 2 * k) if k else rows for k in range(chips)]
        if c < CHUNKS - 1:
            swapped = over_token(jnp.concatenate(there, axis=0), 1)
            blocks = there + [swapped[k * span : (k + 1) * span] for k in range(chips)]
            total = first_mix(at, weights[c], blocks)
        else:
            last = [over_token(there[0], 1)]
            last += [over_token(r, 1) for r in there[1:]]
            blocks = there + last
    return last_mix(at, weights[-1], total, blocks)


def solution(mesh):
    placed = (
        P(("batch", "token"), None),
        P(),
        P("token", None, "batch"),
        P("token", "batch", None),
    )

    return jax.shard_map(
        body, mesh=mesh, in_specs=placed, out_specs=P(("batch", "token"), None), check_vma=False
    )
```

```python
import functools

import jax
import jax.numpy as jnp
from jax import lax
from jax.experimental import pallas as pl
from jax.experimental.pallas import tpu as pltpu
from jax.sharding import PartitionSpec as P


F32, BF16 = jnp.float32, jnp.bfloat16
CHUNKS = 2
HINTS = (1e11, 1e11, 1e11, 1e6, 1e6)
STATS = 8
EXPERT_HINT = 1e9


def in_vmem(x):
    return pltpu.with_memory_space_constraint(x, pltpu.VMEM)


def call(kernel, shapes, operands, *, moved, scalars=0, scratch=(), dtype=BF16, hint=1e11, limit=8 << 20):
    many = isinstance(shapes, list)
    shapes = shapes if many else [shapes]
    scalar, place = pl.BlockSpec(memory_space=pltpu.SMEM), pl.BlockSpec(memory_space=pltpu.VMEM)
    results = pl.pallas_call(
        kernel,
        out_shape=[pltpu.VMEM(shape, dtype) for shape in shapes],
        in_specs=[scalar] * scalars + [place] * (len(operands) - scalars),
        out_specs=[place] * len(shapes),
        scratch_shapes=scratch,
        cost_estimate=pl.CostEstimate(flops=int(hint), bytes_accessed=int(moved), transcendentals=0),
        compiler_params=pltpu.CompilerParams(vmem_limit_bytes=limit),
    )(*operands[:scalars], *[in_vmem(x) for x in operands[scalars:]])
    return results if many else results[0]


def normalize_kernel(x_ref, out_ref):
    x = x_ref[...].astype(F32)
    scale = lax.rsqrt(jnp.mean(x * x, axis=-1, keepdims=True) + 1e-06)
    out_ref[...] = (x * scale).astype(BF16)


def normalize(x):
    return call(normalize_kernel, x.shape, [x], moved=4 * x.size)


def partial_kernel(slots, count, *refs):
    which_refs, (own_ref, other_ref, w_ref), out_refs = refs[:count], refs[count : count + 3], refs[count + 3 :]
    span = out_refs[0].shape[0] - STATS
    if len(w_ref.shape) == 2:
        columns = [
            w_ref[:, pl.ds(pl.multiple_of(which_refs[n][0] * slots, slots), slots)]
            for n in range(count)
        ]
    else:
        columns = [w_ref[which_refs[n][0]] for n in range(count)]
    w = jnp.concatenate(columns, axis=1)
    own, other = own_ref[...], other_ref[...]
    l0 = jnp.dot(own, w, preferred_element_type=F32)
    l1 = jnp.dot(other, w, preferred_element_type=F32)
    top = jnp.maximum(jnp.max(l0, axis=0, keepdims=True), jnp.max(l1, axis=0, keepdims=True))
    top = top.astype(BF16).astype(F32)
    e0, e1 = jnp.exp(l0 - top), jnp.exp(l1 - top)
    total = jnp.sum(e0, axis=0, keepdims=True) + jnp.sum(e1, axis=0, keepdims=True)
    dims = (((0,), (0,)), ((), ()))
    value = lax.dot_general(e0.astype(BF16), own, dims, preferred_element_type=F32)
    value += lax.dot_general(e1.astype(BF16), other, dims, preferred_element_type=F32)
    high = total.astype(BF16).astype(F32)
    row = lax.broadcasted_iota(jnp.int32, (STATS, w.shape[1]), 0)
    stats = jnp.where(row == 0, top, jnp.where(row == 1, high, total - high)).astype(BF16)
    value = value.astype(BF16)
    for n, out_ref in enumerate(out_refs):
        part = slice(n * span, (n + 1) * span)
        out_ref[:span, :] = value[part]
        out_ref[span:, :] = jnp.zeros((STATS, out_ref.shape[1]), BF16)
        out_ref[span:, :span] = stats[:, part]


def partial(which, own, other, weight, slots, chunks, hint):
    rows, width = own.shape
    return call(
        functools.partial(partial_kernel, slots, len(which)),
        [(slots // chunks + STATS, width)] * (len(which) * chunks),
        [*which, own, other, weight],
        moved=4 * rows * width,
        scalars=len(which),
        hint=hint,
        limit=(2 + 5 * max(1, len(which) * slots // 128)) << 20,
    )


def combine_kernel(count, *refs):
    parts, out_refs = refs[:count], refs[count:]
    span = out_refs[0].shape[0]
    slots = span * len(out_refs)
    tops = [p[slots : slots + 1, :slots].astype(F32) for p in parts]
    totals = [
        p[slots + 1 : slots + 2, :slots].astype(F32) + p[slots + 2 : slots + 3, :slots].astype(F32)
        for p in parts
    ]
    top = functools.reduce(jnp.maximum, tops)
    factors = [jnp.exp(t - top) for t in tops]
    total = sum(f * t for f, t in zip(factors, totals))
    inverse = 1.0 / total
    shape = (slots, slots)
    eye = lax.broadcasted_iota(jnp.int32, shape, 0) == lax.broadcasted_iota(jnp.int32, shape, 1)
    value = 0.0
    for f, p in zip(factors, parts):
        column = jnp.sum(jnp.where(eye, f * inverse, 0.0), axis=1, keepdims=True)
        value = value + p[:slots, :].astype(F32) * column
    value = value.astype(BF16)
    for n, out_ref in enumerate(out_refs):
        out_ref[...] = value[n * span : (n + 1) * span]


def combine(parts, slots, chunks):
    width = parts[0].shape[1]
    return call(
        functools.partial(combine_kernel, len(parts)),
        [(slots // chunks, width)] * chunks,
        parts,
        moved=2 * len(parts) * slots * width,
        hint=HINTS[4],
    )


def softmax_kernel(step, span, x_ref, w_ref, *out_refs):
    chunks = len(out_refs)

    @pl.loop(0, x_ref.shape[0] // step)
    def _(i):
        rows = pl.ds(pl.multiple_of(i * step, step), step)
        logits = jnp.dot(x_ref[rows, :], w_ref[...], preferred_element_type=F32)
        raised = jnp.exp(logits - jnp.max(logits, axis=1, keepdims=True))
        share = raised / jnp.sum(raised, axis=1, keepdims=True)
        for c, out_ref in enumerate(out_refs):
            pieces = [
                share[:, at : at + span] for at in range(c * span, share.shape[1], chunks * span)
            ]
            out_ref[rows, :] = jnp.concatenate(pieces, axis=1).astype(BF16)


def softmax(x, weight, span, chunks):
    rows, width = x.shape
    slots = weight.shape[1]
    return call(
        functools.partial(softmax_kernel, min(rows, 256), span),
        [(rows, slots // chunks)] * chunks,
        [x, weight],
        moved=2 * (rows * width + width * slots + rows * slots),
        hint=HINTS[3],
    )


def expert_kernel(count, first, n, each, *refs):
    xs, w_in, w_out, ys = refs[:count], refs[count], refs[count + 1], refs[count + 2 :]

    @pl.loop(0, n)
    def _(e):
        at = pl.ds(pl.multiple_of(e * each, each), each)
        rows = jnp.concatenate([x[at, :] for x in xs], axis=0)
        hidden = jnp.dot(rows, w_in[first + e], preferred_element_type=F32)
        hidden = (0.5 * hidden * (1.0 + lax.erf(hidden * 0.7071067811865476))).astype(BF16)
        terms = jnp.dot(hidden, w_out[first + e], preferred_element_type=F32)
        for k, y in enumerate(ys):
            y[at, :] = terms[k * each : (k + 1) * each].astype(BF16)


def experts(xs, w_in, w_out, first, count):
    rows, width = xs[0].shape
    return call(
        functools.partial(expert_kernel, len(xs), first, count, rows // count),
        [(rows, width)] * len(xs),
        [*xs, w_in, w_out],
        moved=1,
        hint=EXPERT_HINT,
        limit=4 << 20,
    )


def total_kernel(count, *refs):
    refs[count][...] = sum(r[...].astype(F32) for r in refs[:count]).astype(BF16)


def add_up(parts):
    rows, width = parts[0].shape
    return call(
        functools.partial(total_kernel, len(parts)),
        (rows, width),
        parts,
        moved=2 * len(parts) * rows * width,
    )


def place_rows(at_ref, blocks, held):
    span = blocks[0].shape[0]
    for j, block in enumerate(blocks):
        held[pl.ds(pl.multiple_of(at_ref[j] * span, 8), span), :] = block[...]


def first_mix_kernel(at_ref, c_ref, *refs):
    *blocks, out_ref, held = refs
    place_rows(at_ref, blocks, held)
    out_ref[...] = jnp.dot(c_ref[...], held[...], preferred_element_type=F32)


def last_mix_kernel(steps, at_ref, c_ref, sum_ref, *refs):
    *blocks, out_ref, held, made, sems = refs
    place_rows(at_ref, blocks, held)
    step = c_ref.shape[0] // steps
    copies = []
    for i in range(steps):
        rows = pl.ds(i * step, step)
        total = sum_ref[rows, :] + jnp.dot(c_ref[rows, :], held[...], preferred_element_type=F32)
        made[rows, :] = total.astype(BF16)
        copies.append(pltpu.make_async_copy(made.at[rows, :], out_ref.at[rows, :], sems.at[i]))
        copies[-1].start()
    for copy in copies:
        copy.wait()


def first_mix(at, weights, blocks):
    rows, slots = weights.shape
    width = blocks[0].shape[1]
    return call(
        first_mix_kernel,
        (rows, width),
        [at, weights, *blocks],
        moved=2 * (rows * slots + slots * width + rows * width),
        scalars=1,
        scratch=[pltpu.VMEM((slots, width), BF16)],
        dtype=F32,
    )


def last_mix(at, weights, before, blocks):
    rows, slots = weights.shape
    width = blocks[0].shape[1]
    steps = 4
    place = pl.BlockSpec(memory_space=pltpu.VMEM)
    return pl.pallas_call(
        functools.partial(last_mix_kernel, steps),
        out_shape=jax.ShapeDtypeStruct((rows, width), BF16),
        in_specs=[pl.BlockSpec(memory_space=pltpu.SMEM)] + [place] * (len(blocks) + 2),
        out_specs=pl.BlockSpec(memory_space=pl.ANY),
        scratch_shapes=[
            pltpu.VMEM((slots, width), BF16),
            pltpu.VMEM((rows, width), BF16),
            pltpu.SemaphoreType.DMA((steps,)),
        ],
        compiler_params=pltpu.CompilerParams(vmem_limit_bytes=8 << 20),
        name="last_mix",
    )(at, in_vmem(weights), in_vmem(before), *[in_vmem(b) for b in blocks])


def body(tokens, slot_weight, expert_in, expert_out):
    n_token, n_batch = lax.axis_size("token"), lax.axis_size("batch")
    me = lax.axis_index("token")
    chips = n_token // 2
    experts_here = expert_in.shape[0]
    slots = slot_weight.shape[1] // n_token
    width = tokens.shape[1]
    chunk_experts, span = experts_here // CHUNKS, slots // CHUNKS

    def over_token(x, k):
        return lax.ppermute(x, "token", [(i, i ^ k) for i in range(n_token)])

    def over_batch(x, k):
        return lax.ppermute(x, "batch", [(i, i ^ k) for i in range(n_batch)])

    other = normalize(over_token(tokens, 1))
    own = normalize(tokens)
    if slots % 128:
        weight = slot_weight.reshape(width, n_token, slots).transpose(1, 0, 2)
    else:
        weight = slot_weight
    away = list(reversed(range(1, chips)))
    made = [[] for _ in range(CHUNKS)]
    for n, ks in enumerate((away[:1], away[1:], [0])):
        which = [jnp.bitwise_xor(me, 2 * k).astype(jnp.int32)[None] for k in ks]
        results = partial(which, own, other, weight, slots, CHUNKS, HINTS[n])
        for c in range(CHUNKS):
            made[c] += [(k, results[i * CHUNKS + c]) for i, k in enumerate(ks)]
    inputs = []
    for c in range(CHUNKS):
        arrived = [over_token(x, 2 * k) if k else x for k, x in made[c]]
        inputs += combine(arrived, span, 1)
    weights = softmax(own, slot_weight, span, CHUNKS)

    order = [2 * k for k in range(chips)] + [2 * k + 1 for k in range(chips)]
    at = jnp.bitwise_xor(me, jnp.array(order, jnp.int32))
    xs = []
    for x in inputs:
        held = {0: x}
        bit = n_batch // 2
        while bit:
            for k in list(held):
                held[k ^ bit] = over_batch(held[k], bit)
            bit //= 2
        xs.append([held[k] for k in range(n_batch)])
    keys = list(range(n_batch))
    total, parts = None, []
    for c in range(CHUNKS):
        ys = experts(xs[c], expert_in, expert_out, c * chunk_experts, chunk_experts)
        parts.append([over_batch(ys[k], k) if k else ys[k] for k in reversed(keys)])
    for c in range(CHUNKS):
        rows = add_up(parts[c])
        there = [over_token(rows, 2 * k) if k else rows for k in range(chips)]
        swapped = [over_token(there[0], 1)]
        swapped += [over_token(r, 1) for r in there[1:]]
        blocks = there + swapped
        if c < CHUNKS - 1:
            total = first_mix(at, weights[c], blocks)
    return last_mix(at, weights[-1], total, blocks)


def solution(mesh):
    placed = (
        P(("batch", "token"), None),
        P(),
        P("token", None, "batch"),
        P("token", "batch", None),
    )

    return jax.shard_map(
        body, mesh=mesh, in_specs=placed, out_specs=P(("batch", "token"), None), check_vma=False
    )
```

```python
import functools

import jax
import jax.numpy as jnp
from jax import lax
from jax.experimental import pallas as pl
from jax.experimental.pallas import tpu as pltpu
from jax.sharding import PartitionSpec as P


F32, BF16 = jnp.float32, jnp.bfloat16
SHARE = 0.5
RELAYED = (True, False)
HINTS = (1e11, 1e11, 1e6, 1e6, 1e6)
STATS = 8
EXPERT_HINT = 1e9


def in_vmem(x):
    return pltpu.with_memory_space_constraint(x, pltpu.VMEM)


def call(kernel, shapes, operands, *, moved, scalars=0, scratch=(), dtype=BF16, hint=1e11, limit=8 << 20):
    many = isinstance(shapes, list)
    shapes = shapes if many else [shapes]
    scalar, place = pl.BlockSpec(memory_space=pltpu.SMEM), pl.BlockSpec(memory_space=pltpu.VMEM)
    results = pl.pallas_call(
        kernel,
        out_shape=[pltpu.VMEM(shape, dtype) for shape in shapes],
        in_specs=[scalar] * scalars + [place] * (len(operands) - scalars),
        out_specs=[place] * len(shapes),
        scratch_shapes=scratch,
        cost_estimate=pl.CostEstimate(flops=int(hint), bytes_accessed=int(moved), transcendentals=0),
        compiler_params=pltpu.CompilerParams(vmem_limit_bytes=limit),
    )(*operands[:scalars], *[in_vmem(x) for x in operands[scalars:]])
    return results if many else results[0]


def normalize_kernel(x_ref, out_ref):
    x = x_ref[...].astype(F32)
    scale = lax.rsqrt(jnp.mean(x * x, axis=-1, keepdims=True) + 1e-06)
    out_ref[...] = (x * scale).astype(BF16)


def normalize(x):
    return call(normalize_kernel, x.shape, [x], moved=4 * x.size)


def partial_kernel(slots, count, *refs):
    which_refs, (own_ref, other_ref, w_ref), out_refs = refs[:count], refs[count : count + 3], refs[count + 3 :]
    if len(w_ref.shape) == 2:
        columns = [
            w_ref[:, pl.ds(pl.multiple_of(which_refs[n][0] * slots, slots), slots)]
            for n in range(count)
        ]
    else:
        columns = [w_ref[which_refs[n][0]] for n in range(count)]
    w = jnp.concatenate(columns, axis=1)
    own, other = own_ref[...], other_ref[...]
    l0 = jnp.dot(own, w, preferred_element_type=F32)
    l1 = jnp.dot(other, w, preferred_element_type=F32)
    top = jnp.maximum(jnp.max(l0, axis=0, keepdims=True), jnp.max(l1, axis=0, keepdims=True))
    top = top.astype(BF16).astype(F32)
    e0, e1 = jnp.exp(l0 - top), jnp.exp(l1 - top)
    total = jnp.sum(e0, axis=0, keepdims=True) + jnp.sum(e1, axis=0, keepdims=True)
    dims = (((0,), (0,)), ((), ()))
    value = lax.dot_general(e0.astype(BF16), own, dims, preferred_element_type=F32)
    value += lax.dot_general(e1.astype(BF16), other, dims, preferred_element_type=F32)
    high = total.astype(BF16).astype(F32)
    row = lax.broadcasted_iota(jnp.int32, (STATS, w.shape[1]), 0)
    stats = jnp.where(row == 0, top, jnp.where(row == 1, high, total - high)).astype(BF16)
    value = value.astype(BF16)
    at = 0
    for out_ref in out_refs:
        span = out_ref.shape[0] - STATS
        part = slice(at, at + span)
        out_ref[:span, :] = value[part]
        out_ref[span:, :] = jnp.zeros((STATS, out_ref.shape[1]), BF16)
        out_ref[span:, :span] = stats[:, part]
        at += span


def partial(which, own, other, weight, spans, hint):
    slots = sum(spans)
    rows, width = own.shape
    return call(
        functools.partial(partial_kernel, slots, len(which)),
        [(span + STATS, width) for span in spans] * len(which),
        [*which, own, other, weight],
        moved=4 * rows * width,
        scalars=len(which),
        hint=hint,
        limit=(2 + 5 * max(1, len(which) * slots // 128)) << 20,
    )


def combine_kernel(count, *refs):
    parts, out_refs = refs[:count], refs[count:]
    span = out_refs[0].shape[0]
    slots = span * len(out_refs)
    tops = [p[slots : slots + 1, :slots].astype(F32) for p in parts]
    totals = [
        p[slots + 1 : slots + 2, :slots].astype(F32) + p[slots + 2 : slots + 3, :slots].astype(F32)
        for p in parts
    ]
    top = functools.reduce(jnp.maximum, tops)
    factors = [jnp.exp(t - top) for t in tops]
    total = sum(f * t for f, t in zip(factors, totals))
    inverse = 1.0 / total
    shape = (slots, slots)
    eye = lax.broadcasted_iota(jnp.int32, shape, 0) == lax.broadcasted_iota(jnp.int32, shape, 1)
    value = 0.0
    for f, p in zip(factors, parts):
        column = jnp.sum(jnp.where(eye, f * inverse, 0.0), axis=1, keepdims=True)
        value = value + p[:slots, :].astype(F32) * column
    value = value.astype(BF16)
    for n, out_ref in enumerate(out_refs):
        out_ref[...] = value[n * span : (n + 1) * span]


def combine(parts, slots, chunks):
    width = parts[0].shape[1]
    return call(
        functools.partial(combine_kernel, len(parts)),
        [(slots // chunks, width)] * chunks,
        parts,
        moved=2 * len(parts) * slots * width,
        hint=HINTS[4],
    )


def softmax_kernel(step, spans, x_ref, w_ref, *out_refs):
    slots = sum(spans)

    @pl.loop(0, x_ref.shape[0] // step)
    def _(i):
        rows = pl.ds(pl.multiple_of(i * step, step), step)
        logits = jnp.dot(x_ref[rows, :], w_ref[...], preferred_element_type=F32)
        raised = jnp.exp(logits - jnp.max(logits, axis=1, keepdims=True))
        share = raised / jnp.sum(raised, axis=1, keepdims=True)
        first = 0
        for span, out_ref in zip(spans, out_refs):
            pieces = [
                share[:, at : at + span] for at in range(first, share.shape[1], slots)
            ]
            out_ref[rows, :] = jnp.concatenate(pieces, axis=1).astype(BF16)
            first += span


def softmax(x, weight, spans):
    rows, width = x.shape
    slots = weight.shape[1]
    return call(
        functools.partial(softmax_kernel, min(rows, 256), spans),
        [(rows, slots // sum(spans) * span) for span in spans],
        [x, weight],
        moved=2 * (rows * width + width * slots + rows * slots),
        hint=HINTS[3],
    )


def marker_kernel(x_ref, out_ref):
    out_ref[...] = x_ref[:8, :]


def marker(x):
    return call(marker_kernel, (8, x.shape[1]), [x], moved=1, hint=1e11, limit=1 << 20)


def expert_kernel(count, first, n, each, *refs):
    xs, w_in, w_out, ys = refs[:count], refs[count], refs[count + 1], refs[count + 3 :]

    @pl.loop(0, n)
    def _(e):
        at = pl.ds(pl.multiple_of(e * each, each), each)
        rows = jnp.concatenate([x[at, :] for x in xs], axis=0)
        hidden = jnp.dot(rows, w_in[first + e], preferred_element_type=F32)
        hidden = (0.5 * hidden * (1.0 + lax.erf(hidden * 0.7071067811865476))).astype(BF16)
        terms = jnp.dot(hidden, w_out[first + e], preferred_element_type=F32)
        for k, y in enumerate(ys):
            y[at, :] = terms[k * each : (k + 1) * each].astype(BF16)


def experts(xs, w_in, w_out, mark, first, count):
    rows, width = xs[0].shape
    return call(
        functools.partial(expert_kernel, len(xs), first, count, rows // count),
        [(rows, width)] * len(xs),
        [*xs, w_in, w_out, mark],
        moved=1,
        hint=EXPERT_HINT,
        limit=4 << 20,
    )


def total_kernel(count, *refs):
    refs[count][...] = sum(r[...].astype(F32) for r in refs[:count]).astype(BF16)


def add_up(parts):
    rows, width = parts[0].shape
    return call(
        functools.partial(total_kernel, len(parts)),
        (rows, width),
        parts,
        moved=2 * len(parts) * rows * width,
    )


def place_rows(at_ref, blocks, held):
    span = blocks[0].shape[0]
    for j, block in enumerate(blocks):
        held[pl.ds(pl.multiple_of(at_ref[j] * span, 8), span), :] = block[...]


def first_mix_kernel(at_ref, c_ref, *refs):
    *blocks, out_ref, held = refs
    place_rows(at_ref, blocks, held)
    out_ref[...] = jnp.dot(c_ref[...], held[...], preferred_element_type=F32)


def last_mix_kernel(steps, at_ref, c_ref, sum_ref, *refs):
    *blocks, out_ref, held, made, sems = refs
    place_rows(at_ref, blocks, held)
    step = c_ref.shape[0] // steps
    copies = []
    for i in range(steps):
        rows = pl.ds(i * step, step)
        total = sum_ref[rows, :] + jnp.dot(c_ref[rows, :], held[...], preferred_element_type=F32)
        made[rows, :] = total.astype(BF16)
        copies.append(pltpu.make_async_copy(made.at[rows, :], out_ref.at[rows, :], sems.at[i]))
        copies[-1].start()
    for copy in copies:
        copy.wait()


def first_mix(at, weights, blocks):
    rows, slots = weights.shape
    width = blocks[0].shape[1]
    return call(
        first_mix_kernel,
        (rows, width),
        [at, weights, *blocks],
        moved=2 * (rows * slots + slots * width + rows * width),
        scalars=1,
        scratch=[pltpu.VMEM((slots, width), BF16)],
        dtype=F32,
    )


def last_mix(at, weights, before, blocks):
    rows, slots = weights.shape
    width = blocks[0].shape[1]
    steps = 4
    place = pl.BlockSpec(memory_space=pltpu.VMEM)
    return pl.pallas_call(
        functools.partial(last_mix_kernel, steps),
        out_shape=jax.ShapeDtypeStruct((rows, width), BF16),
        in_specs=[pl.BlockSpec(memory_space=pltpu.SMEM)] + [place] * (len(blocks) + 2),
        out_specs=pl.BlockSpec(memory_space=pl.ANY),
        scratch_shapes=[
            pltpu.VMEM((slots, width), BF16),
            pltpu.VMEM((rows, width), BF16),
            pltpu.SemaphoreType.DMA((steps,)),
        ],
        compiler_params=pltpu.CompilerParams(vmem_limit_bytes=8 << 20),
        name="last_mix",
    )(at, in_vmem(weights), in_vmem(before), *[in_vmem(b) for b in blocks])


def body(tokens, slot_weight, expert_in, expert_out):
    n_token, n_batch = lax.axis_size("token"), lax.axis_size("batch")
    me = lax.axis_index("token")
    chips = n_token // 2
    experts_here = expert_in.shape[0]
    slots = slot_weight.shape[1] // n_token
    width = tokens.shape[1]
    first = max(1, min(experts_here - 1, round(experts_here * SHARE)))
    counts = [first, experts_here - first]
    spans = [n * (slots // experts_here) for n in counts]
    chunks = len(counts)

    def over_token(x, k):
        return lax.ppermute(x, "token", [(i, i ^ k) for i in range(n_token)])

    def over_batch(x, k):
        return lax.ppermute(x, "batch", [(i, i ^ k) for i in range(n_batch)])

    other = normalize(over_token(tokens, 1))
    own = normalize(tokens)
    if slots % 128:
        weight = slot_weight.reshape(width, n_token, slots).transpose(1, 0, 2)
    else:
        weight = slot_weight
    away = list(reversed(range(1, chips)))
    made = [[] for _ in range(chunks)]
    for n, ks in enumerate((away[:1], away[1:], [0])):
        which = [jnp.bitwise_xor(me, 2 * k).astype(jnp.int32)[None] for k in ks]
        results = partial(which, own, other, weight, spans, HINTS[n])
        for c in range(chunks):
            made[c] += [(k, results[i * chunks + c]) for i, k in enumerate(ks)]
    inputs = []
    for c in range(chunks):
        arrived = [over_token(x, 2 * k) if k else x for k, x in made[c]]
        inputs += combine(arrived, spans[c], 1)
    mark = marker(inputs[0])
    weights = softmax(own, slot_weight, spans)

    order = [2 * k for k in range(chips)] + [2 * k + 1 for k in range(chips)]
    at = jnp.bitwise_xor(me, jnp.array(order, jnp.int32))
    xs = []
    for c, x in enumerate(inputs):
        held = {0: x}
        if RELAYED[c]:
            bit = n_batch // 2
            while bit:
                for k in list(held):
                    held[k ^ bit] = over_batch(held[k], bit)
                bit //= 2
        else:
            for k in reversed(range(1, n_batch)):
                held[k] = over_batch(x, k)
        xs.append([held[k] for k in range(n_batch)])
    keys = list(range(n_batch))
    total, parts = None, []
    for c in range(chunks):
        ys = experts(xs[c], expert_in, expert_out, mark, sum(counts[:c]), counts[c])
        parts.append([over_batch(ys[k], k) if k else ys[k] for k in reversed(keys)])
    for c in range(chunks):
        rows = add_up(parts[c])
        there = [rows]
        for k in range(1, chips):
            there.append(over_token(rows, 2 * k))
        swapped = [over_token(there[0], 1)]
        swapped += [over_token(r, 1) for r in there[1:]]
        blocks = there + swapped
        if c < chunks - 1:
            total = first_mix(at, weights[c], blocks)
    return last_mix(at, weights[-1], total, blocks)


def solution(mesh):
    placed = (
        P(("batch", "token"), None),
        P(),
        P("token", None, "batch"),
        P("token", "batch", None),
    )

    return jax.shard_map(
        body, mesh=mesh, in_specs=placed, out_specs=P(("batch", "token"), None), check_vma=False
    )
```

```python
import functools

import jax
import jax.numpy as jnp
from jax import lax
from jax.experimental import pallas as pl
from jax.experimental.pallas import tpu as pltpu
from jax.sharding import PartitionSpec as P


F32, BF16 = jnp.float32, jnp.bfloat16
SHARE = 0.5
RELAYED = (True, False)
HINTS = (1e11, 1e11, 1e6, 1e6, 1e6)
STATS = 8
UNROLL = 4
EXPERT_HINT = 1e9


def in_vmem(x):
    return pltpu.with_memory_space_constraint(x, pltpu.VMEM)


def call(kernel, shapes, operands, *, moved, scalars=0, scratch=(), dtype=BF16, hint=1e11, limit=8 << 20):
    many = isinstance(shapes, list)
    shapes = shapes if many else [shapes]
    scalar, place = pl.BlockSpec(memory_space=pltpu.SMEM), pl.BlockSpec(memory_space=pltpu.VMEM)
    results = pl.pallas_call(
        kernel,
        out_shape=[pltpu.VMEM(shape, dtype) for shape in shapes],
        in_specs=[scalar] * scalars + [place] * (len(operands) - scalars),
        out_specs=[place] * len(shapes),
        scratch_shapes=scratch,
        cost_estimate=pl.CostEstimate(flops=int(hint), bytes_accessed=int(moved), transcendentals=0),
        compiler_params=pltpu.CompilerParams(vmem_limit_bytes=limit),
    )(*operands[:scalars], *[in_vmem(x) for x in operands[scalars:]])
    return results if many else results[0]


def normalize_kernel(x_ref, out_ref):
    x = x_ref[...].astype(F32)
    scale = lax.rsqrt(jnp.mean(x * x, axis=-1, keepdims=True) + 1e-06)
    out_ref[...] = (x * scale).astype(BF16)


def normalize(x, hint):
    return call(normalize_kernel, x.shape, [x], moved=4 * x.size, hint=hint)


def partial_kernel(slots, count, *refs):
    which_refs, (own_ref, other_ref, w_ref), out_refs = refs[:count], refs[count : count + 3], refs[count + 3 :]
    if len(w_ref.shape) == 2:
        columns = [
            w_ref[:, pl.ds(pl.multiple_of(which_refs[n][0] * slots, slots), slots)]
            for n in range(count)
        ]
    else:
        columns = [w_ref[which_refs[n][0]] for n in range(count)]
    w = jnp.concatenate(columns, axis=1)
    own, other = own_ref[...], other_ref[...]
    l0 = jnp.dot(own, w, preferred_element_type=F32)
    l1 = jnp.dot(other, w, preferred_element_type=F32)
    top = jnp.maximum(jnp.max(l0, axis=0, keepdims=True), jnp.max(l1, axis=0, keepdims=True))
    top = top.astype(BF16).astype(F32)
    e0, e1 = jnp.exp(l0 - top), jnp.exp(l1 - top)
    total = jnp.sum(e0, axis=0, keepdims=True) + jnp.sum(e1, axis=0, keepdims=True)
    dims = (((0,), (0,)), ((), ()))
    value = lax.dot_general(e0.astype(BF16), own, dims, preferred_element_type=F32)
    value += lax.dot_general(e1.astype(BF16), other, dims, preferred_element_type=F32)
    high = total.astype(BF16).astype(F32)
    row = lax.broadcasted_iota(jnp.int32, (STATS, w.shape[1]), 0)
    stats = jnp.where(row == 0, top, jnp.where(row == 1, high, total - high)).astype(BF16)
    value = value.astype(BF16)
    at = 0
    for out_ref in out_refs:
        span = out_ref.shape[0] - STATS
        part = slice(at, at + span)
        out_ref[:span, :] = value[part]
        out_ref[span:, :] = jnp.zeros((STATS, out_ref.shape[1]), BF16)
        out_ref[span:, :span] = stats[:, part]
        at += span


def partial(which, own, other, weight, spans, hint):
    slots = sum(spans)
    rows, width = own.shape
    return call(
        functools.partial(partial_kernel, slots, len(which)),
        [(span + STATS, width) for span in spans] * len(which),
        [*which, own, other, weight],
        moved=4 * rows * width,
        scalars=len(which),
        hint=hint,
        limit=(2 + 5 * max(1, len(which) * slots // 128)) << 20,
    )


def combine_kernel(count, *refs):
    parts, out_refs = refs[:count], refs[count:]
    span = out_refs[0].shape[0]
    slots = span * len(out_refs)
    tops = [p[slots : slots + 1, :slots].astype(F32) for p in parts]
    totals = [
        p[slots + 1 : slots + 2, :slots].astype(F32) + p[slots + 2 : slots + 3, :slots].astype(F32)
        for p in parts
    ]
    top = functools.reduce(jnp.maximum, tops)
    factors = [jnp.exp(t - top) for t in tops]
    total = sum(f * t for f, t in zip(factors, totals))
    inverse = 1.0 / total
    shape = (slots, slots)
    eye = lax.broadcasted_iota(jnp.int32, shape, 0) == lax.broadcasted_iota(jnp.int32, shape, 1)
    value = 0.0
    for f, p in zip(factors, parts):
        column = jnp.sum(jnp.where(eye, f * inverse, 0.0), axis=1, keepdims=True)
        value = value + p[:slots, :].astype(F32) * column
    value = value.astype(BF16)
    for n, out_ref in enumerate(out_refs):
        out_ref[...] = value[n * span : (n + 1) * span]


def combine(parts, slots, chunks):
    width = parts[0].shape[1]
    return call(
        functools.partial(combine_kernel, len(parts)),
        [(slots // chunks, width)] * chunks,
        parts,
        moved=2 * len(parts) * slots * width,
        hint=HINTS[4],
    )


def softmax_kernel(step, spans, x_ref, w_ref, *out_refs):
    slots = sum(spans)

    @pl.loop(0, x_ref.shape[0] // step)
    def _(i):
        rows = pl.ds(pl.multiple_of(i * step, step), step)
        logits = jnp.dot(x_ref[rows, :], w_ref[...], preferred_element_type=F32)
        raised = jnp.exp(logits - jnp.max(logits, axis=1, keepdims=True))
        share = raised / jnp.sum(raised, axis=1, keepdims=True)
        first = 0
        for span, out_ref in zip(spans, out_refs):
            pieces = [
                share[:, at : at + span] for at in range(first, share.shape[1], slots)
            ]
            out_ref[rows, :] = jnp.concatenate(pieces, axis=1).astype(BF16)
            first += span


def softmax(x, weight, spans):
    rows, width = x.shape
    slots = weight.shape[1]
    return call(
        functools.partial(softmax_kernel, min(rows, 256), spans),
        [(rows, slots // sum(spans) * span) for span in spans],
        [x, weight],
        moved=2 * (rows * width + width * slots + rows * slots),
        hint=HINTS[3],
    )


def marker_kernel(x_ref, out_ref):
    out_ref[...] = x_ref[:8, :]


def marker(x):
    return call(marker_kernel, (8, x.shape[1]), [x], moved=1, hint=1e11, limit=1 << 20)


def expert_kernel(count, first, n, each, *refs):
    xs, w_in, w_out, ys = refs[:count], refs[count], refs[count + 1], refs[count + 3 :]

    group = next(g for g in (UNROLL, 2, 1) if n % g == 0)

    @pl.loop(0, n // group)
    def _(step):
        hiddens = []
        for i in range(group):
            e = step * group + i
            at = pl.ds(pl.multiple_of(e * each, each), each)
            rows = jnp.concatenate([x[at, :] for x in xs], axis=0)
            hidden = jnp.dot(rows, w_in[first + e], preferred_element_type=F32)
            hidden = 0.5 * hidden * (1.0 + lax.erf(hidden * 0.7071067811865476))
            hiddens.append(hidden.astype(BF16))
        for i, hidden in enumerate(hiddens):
            e = step * group + i
            at = pl.ds(pl.multiple_of(e * each, each), each)
            terms = jnp.dot(hidden, w_out[first + e], preferred_element_type=F32)
            for k, y in enumerate(ys):
                y[at, :] = terms[k * each : (k + 1) * each].astype(BF16)


def experts(xs, w_in, w_out, mark, first, count):
    rows, width = xs[0].shape
    return call(
        functools.partial(expert_kernel, len(xs), first, count, rows // count),
        [(rows, width)] * len(xs),
        [*xs, w_in, w_out, mark],
        moved=1,
        hint=EXPERT_HINT,
        limit=4 << 20,
    )


def total_kernel(count, *refs):
    refs[count][...] = sum(r[...].astype(F32) for r in refs[:count]).astype(BF16)


def add_up(parts):
    rows, width = parts[0].shape
    return call(
        functools.partial(total_kernel, len(parts)),
        (rows, width),
        parts,
        moved=2 * len(parts) * rows * width,
    )


def place_rows(at_ref, blocks, held):
    span = blocks[0].shape[0]
    for j, block in enumerate(blocks):
        held[pl.ds(pl.multiple_of(at_ref[j] * span, 8), span), :] = block[...]


def first_mix_kernel(at_ref, c_ref, *refs):
    *blocks, out_ref, held = refs
    place_rows(at_ref, blocks, held)
    out_ref[...] = jnp.dot(c_ref[...], held[...], preferred_element_type=F32)


def last_mix_kernel(steps, at_ref, c_ref, sum_ref, *refs):
    *blocks, out_ref, held, made, sems = refs
    place_rows(at_ref, blocks, held)
    step = c_ref.shape[0] // steps
    copies = []
    for i in range(steps):
        rows = pl.ds(i * step, step)
        total = sum_ref[rows, :] + jnp.dot(c_ref[rows, :], held[...], preferred_element_type=F32)
        made[rows, :] = total.astype(BF16)
        copies.append(pltpu.make_async_copy(made.at[rows, :], out_ref.at[rows, :], sems.at[i]))
        copies[-1].start()
    for copy in copies:
        copy.wait()


def first_mix(at, weights, blocks):
    rows, slots = weights.shape
    width = blocks[0].shape[1]
    return call(
        first_mix_kernel,
        (rows, width),
        [at, weights, *blocks],
        moved=2 * (rows * slots + slots * width + rows * width),
        scalars=1,
        scratch=[pltpu.VMEM((slots, width), BF16)],
        dtype=F32,
    )


def last_mix(at, weights, before, blocks):
    rows, slots = weights.shape
    width = blocks[0].shape[1]
    steps = 2
    place = pl.BlockSpec(memory_space=pltpu.VMEM)
    return pl.pallas_call(
        functools.partial(last_mix_kernel, steps),
        out_shape=jax.ShapeDtypeStruct((rows, width), BF16),
        in_specs=[pl.BlockSpec(memory_space=pltpu.SMEM)] + [place] * (len(blocks) + 2),
        out_specs=pl.BlockSpec(memory_space=pl.ANY),
        scratch_shapes=[
            pltpu.VMEM((slots, width), BF16),
            pltpu.VMEM((rows, width), BF16),
            pltpu.SemaphoreType.DMA((steps,)),
        ],
        compiler_params=pltpu.CompilerParams(vmem_limit_bytes=8 << 20),
        name="last_mix",
    )(at, in_vmem(weights), in_vmem(before), *[in_vmem(b) for b in blocks])


def body(tokens, slot_weight, expert_in, expert_out):
    n_token, n_batch = lax.axis_size("token"), lax.axis_size("batch")
    me = lax.axis_index("token")
    chips = n_token // 2
    experts_here = expert_in.shape[0]
    slots = slot_weight.shape[1] // n_token
    width = tokens.shape[1]
    first = max(1, min(experts_here - 1, round(experts_here * SHARE)))
    counts = [first, experts_here - first]
    spans = [n * (slots // experts_here) for n in counts]
    chunks = len(counts)

    def over_token(x, k):
        return lax.ppermute(x, "token", [(i, i ^ k) for i in range(n_token)])

    def over_batch(x, k):
        return lax.ppermute(x, "batch", [(i, i ^ k) for i in range(n_batch)])

    other = normalize(over_token(tokens, 1), 1e6)
    own = normalize(tokens, 1e11)
    if slots % 128:
        weight = slot_weight.reshape(width, n_token, slots).transpose(1, 0, 2)
    else:
        weight = slot_weight
    away = list(reversed(range(1, chips)))
    made = [[] for _ in range(chunks)]
    for n, ks in enumerate((away[:1], away[1:], [0])):
        which = [jnp.bitwise_xor(me, 2 * k).astype(jnp.int32)[None] for k in ks]
        results = partial(which, own, other, weight, spans, HINTS[n])
        for c in range(chunks):
            made[c] += [(k, results[i * chunks + c]) for i, k in enumerate(ks)]
    inputs = []
    for c in range(chunks):
        arrived = [over_token(x, 2 * k) if k else x for k, x in made[c]]
        inputs += combine(arrived, spans[c], 1)
    mark = marker(inputs[0])
    weights = softmax(own, slot_weight, spans)

    order = [2 * k for k in range(chips)] + [2 * k + 1 for k in range(chips)]
    at = jnp.bitwise_xor(me, jnp.array(order, jnp.int32))
    xs = []
    for c, x in enumerate(inputs):
        held = {0: x}
        if RELAYED[c]:
            bit = n_batch // 2
            while bit:
                for k in list(held):
                    held[k ^ bit] = over_batch(held[k], bit)
                bit //= 2
        else:
            for k in reversed(range(1, n_batch)):
                held[k] = over_batch(x, k)
        xs.append([held[k] for k in range(n_batch)])
    keys = list(range(n_batch))
    total, parts = None, []
    for c in range(chunks):
        ys = experts(xs[c], expert_in, expert_out, mark, sum(counts[:c]), counts[c])
        part = []
        for k in keys:
            part.append(over_batch(ys[k], k) if k else ys[k])
        parts.append(part)
    for c in range(chunks):
        rows = add_up(parts[c])
        there = [rows]
        for k in range(1, chips):
            there.append(over_token(rows, 2 * k))
        swapped = [over_token(there[0], 1)]
        swapped += [over_token(r, 1) for r in there[1:]]
        blocks = there + swapped
        if c < chunks - 1:
            total = first_mix(at, weights[c], blocks)
    return last_mix(at, weights[-1], total, blocks)


def solution(mesh):
    placed = (
        P(("batch", "token"), None),
        P(),
        P("token", None, "batch"),
        P("token", "batch", None),
    )

    return jax.shard_map(
        body, mesh=mesh, in_specs=placed, out_specs=P(("batch", "token"), None), check_vma=False
    )
```
